32 devices in a mesh: pipe: 4 (over y, core), ctx: 8 (over z, x).
Axes of the slice: x: 2, y: 2, z: 4, core: 2. Of those that a mesh axis runs over, the one named last changes fastest.
Arguments:
- x_proj: bfloat16 [4, 2, 1024, 2048], P('pipe', None, 'ctx'), may hold values from -6 to 6
- gate_proj: bfloat16 [4, 2, 1024, 2048], P('pipe', None, 'ctx'), may hold values from -6 to 6
- bc_proj: bfloat16 [4, 2, 1024, 1024], P('pipe', None, 'ctx'), may hold values from -6 to 6
- dt_raw: float32 [4, 2, 1024, 64], P('pipe', None, 'ctx'), may hold values from -3 to 16
- decay_rate: float32 [4, 64], P('pipe'), may hold values from 0 to 1
- conv_weight: float32 [4, 4, 3072], P('pipe'), may hold values from -3 to 3
- skip_gain: float32 [4, 64], P('pipe'), may hold values from 0.5 to 1.5
- norm_gain: float32 [4, 2048], P('pipe'), may hold values from 0.1 to 1.9
Outputs:
- mixed_out: bfloat16 [4, 2, 1024, 2048], P('pipe', None, 'ctx')
The draws below stay inside these ranges and needn't reach their ends.
All inputs are finite; a program needn't handle non-finite values.
Results may differ from the reference program's by a relative error of at most 0.0052.
Values may be sent and summed in bfloat16 or wider, within the bound.
A program may use at most 64 MiB of HBM per device.

```python
import math
import jax
import jax.numpy as jnp
from jax import lax

HEADS = 64
HEAD_DIM = 32
GROUPS = 8
STATE = 64
KERNEL = 4
BLOCK = 128
SEQS = 2
LAYERS = 4
SEQUENCE_TOKENS = 1024
HD = 2048
CH = 3072


def draw_dt_raw(key, part):
    random_key_root, random_key_position, random_key_range = jax.random.split(key, 3)
    tensor_dimensions = (LAYERS, SEQS, SEQUENCE_TOKENS, HEADS)
    baseline_result = jnp.clip(0.5 * jax.random.normal(random_key_root, tensor_dimensions, jnp.float32), -3.0, 3.0)
    range_positions = jax.random.randint(random_key_position, (LAYERS, SEQS, 3), 0, SEQUENCE_TOKENS)
    range_token_rows = jnp.any(jnp.arange(SEQUENCE_TOKENS)[None, None, :, None] == range_positions[:, :, None, :], axis=-1)
    token_ranges = jax.random.uniform(random_key_range, tensor_dimensions, jnp.float32, 8.0, 16.0)
    return jnp.where(range_token_rows[..., None], token_ranges, baseline_result)


def draw_decay_rate(key, part):
    fraction = jax.random.uniform(key, (LAYERS, HEADS), jnp.float32)
    low_end = math.log(0.2 / SEQUENCE_TOKENS)
    high_end = math.log(60.0 / SEQUENCE_TOKENS)
    return jnp.exp(low_end + fraction * (high_end - low_end))


def levels(key, extent, pieces, least, high):
    factor_of = 1.0
    for axis_at, blocks in pieces:
        heights = jax.random.uniform(jax.random.fold_in(jax.random.fold_in(key, 6), axis_at), (blocks,), jnp.float32, least / len(pieces), high / len(pieces))
        factor_of = factor_of * jnp.repeat(jnp.exp(heights), extent[axis_at] // blocks).reshape((-1,) + (1,) * (len(extent) - 1 - axis_at))
    return factor_of


def centred(rng, shape, width, bound, cuts=(), held_as=jnp.bfloat16):
    drawn = width * jax.random.normal(rng, shape, jnp.float32)
    if cuts:
        drawn = drawn * levels(rng, shape, cuts, -0.22, 0.18)
    return jnp.clip(drawn, -bound, bound).astype(held_as)


def setup_inputs(seed: int = 0) -> dict:
    key_of = jax.random.split(jax.random.key(seed), 9)
    return {
        "x_proj": centred(key_of[0], (LAYERS, SEQS, SEQUENCE_TOKENS, HD), 1.0, 6.0, ((0, 4), (2, 8))),
        "gate_proj": centred(key_of[1], (LAYERS, SEQS, SEQUENCE_TOKENS, HD), 1.0, 6.0, ((0, 4), (2, 8))),
        "bc_proj": centred(key_of[2], (LAYERS, SEQS, SEQUENCE_TOKENS, 2 * GROUPS * STATE), 1.0, 6.0, ((0, 4), (2, 8))),
        "dt_raw": draw_dt_raw(jax.random.fold_in(key_of[8], 71), 0),
        "decay_rate": draw_decay_rate(jax.random.fold_in(key_of[8], 71), 0),
        "conv_weight": centred(key_of[5], (LAYERS, KERNEL, CH), KERNEL ** -0.5, 3.0, ((0, 4),), jnp.float32),
        "skip_gain": jnp.clip(0.5 + 1.0 * jax.random.uniform(key_of[6], (LAYERS, HEADS), jnp.float32) ** levels(key_of[6], (LAYERS, HEADS), ((0, 4),), -0.2, 0.2), 0.5, 1.5),
        "norm_gain": jnp.clip(1.0 + 0.18 * jax.random.normal(key_of[7], (LAYERS, HD), jnp.float32), 0.1, 1.9),
    }


norm_eps = 1e-05
precise_mode = lax.Precision.HIGHEST

def rounded(value):
    return lax.optimization_barrier(value.astype(jnp.bfloat16)).astype(jnp.float32)

def convolve(inputs, weight, head_rows):
    tap_count = weight.shape[0]
    padded = jnp.concatenate([head_rows, inputs], axis=0)
    length = inputs.shape[0]
    conv_sum = weight[0] * padded[0:length]
    for offset in range(1, tap_count):
        conv_sum = conv_sum + weight[offset] * padded[offset:offset + length]
    return jax.nn.silu(conv_sum)

def block_terms(activated, dt_rows, rates):
    feature_width = HEADS * HEAD_DIM
    bc_width = GROUPS * STATE
    per_group = HEADS // GROUPS
    block_count = activated.shape[0] // BLOCK
    inputs_x = activated[:, :feature_width].reshape(block_count, BLOCK, HEADS, HEAD_DIM)
    inputs_b = activated[:, feature_width:feature_width + bc_width].reshape(block_count, BLOCK, GROUPS, STATE)
    inputs_c = activated[:, feature_width + bc_width:].reshape(block_count, BLOCK, GROUPS, STATE)
    steps_dt = jax.nn.softplus(dt_rows).reshape(block_count, BLOCK, HEADS)
    cumulated = jnp.cumsum(-steps_dt * rates, axis=1)
    scores = jnp.einsum('cign,cjgn->cgij', inputs_c, inputs_b, precision=precise_mode)
    scores = jnp.repeat(scores, per_group, axis=1)
    cumul_heads = jnp.transpose(cumulated, (0, 2, 1))
    lower_mask = jnp.arange(BLOCK)[:, None] >= jnp.arange(BLOCK)[None, :]
    log_gaps = cumul_heads[:, :, :, None] - cumul_heads[:, :, None, :]
    decays = jnp.where(lower_mask, jnp.exp(jnp.where(lower_mask, log_gaps, 0.0)), 0.0)
    dt_heads = jnp.transpose(steps_dt, (0, 2, 1))
    weights = rounded(scores * decays * dt_heads[:, :, None, :])
    diag_out = jnp.einsum('chij,cjhp->cihp', weights, inputs_x, precision=precise_mode)
    block_ends = cumulated[:, -1, :]
    tail_weight = jnp.exp(block_ends[:, None, :] - cumulated) * steps_dt
    keyed_rows = rounded(jnp.repeat(inputs_b, per_group, axis=2) * tail_weight[..., None])
    local_states = jnp.einsum('cqhn,cqhp->chpn', keyed_rows, inputs_x, precision=precise_mode)
    return (inputs_x, inputs_c, cumulated, diag_out, local_states, jnp.exp(block_ends))

def finish(inputs_x, inputs_c, cumulated, diag_out, incoming, skips, gate_rows, gains):
    per_group = HEADS // GROUPS
    state_rows = rounded(incoming)
    off_out = jnp.einsum('cqhn,chpn->cqhp', jnp.repeat(inputs_c, per_group, axis=2), state_rows, precision=precise_mode)
    off_out = off_out * jnp.exp(cumulated)[..., None]
    mixed_sum = diag_out + off_out + skips[None, None, :, None] * inputs_x
    length = mixed_sum.shape[0] * mixed_sum.shape[1]
    feature_width = HEADS * HEAD_DIM
    gated_rows = mixed_sum.reshape(length, feature_width) * jax.nn.silu(gate_rows.astype(jnp.float32))
    grouped = gated_rows.reshape(length, GROUPS, feature_width // GROUPS)
    inv_rms = lax.rsqrt(lax.optimization_barrier(jnp.mean(grouped * grouped, axis=-1, keepdims=True)) + norm_eps)
    return ((grouped * inv_rms).reshape(length, feature_width) * gains).astype(jnp.bfloat16)

def sequence_out(x_rows, prev_rows, bc_rows, dt_rows, gate_rows, rates, weight, skips, gains):
    conv_in = jnp.concatenate([x_rows.astype(jnp.float32) + prev_rows.astype(jnp.float32), bc_rows.astype(jnp.float32)], axis=1)
    head_rows = jnp.zeros((weight.shape[0] - 1, conv_in.shape[1]), jnp.float32)
    activated = rounded(convolve(conv_in, weight, head_rows))
    inputs_x, inputs_c, cumulated, diag_out, local_states, factors = block_terms(activated, dt_rows, rates)

    def advance(held_state, step_pair):
        factor, own_term = step_pair
        return (factor[:, None, None] * held_state + own_term, held_state)
    zero_state = jnp.zeros((HEADS, HEAD_DIM, STATE), jnp.float32)
    final_state, incoming = lax.scan(advance, zero_state, (factors, local_states))
    return finish(inputs_x, inputs_c, cumulated, diag_out, incoming, skips, gate_rows, gains)

def reference(x_proj, gate_proj, bc_proj, dt_raw, decay_rate, conv_weight, skip_gain, norm_gain):
    previous = jnp.zeros((SEQS, SEQUENCE_TOKENS, HEADS * HEAD_DIM), jnp.bfloat16)
    outputs = []
    for layer_idx in range(LAYERS):

        def one_sequence(seq_index, layer_idx=layer_idx, previous=previous):
            return sequence_out(x_proj[layer_idx, seq_index], previous[seq_index], bc_proj[layer_idx, seq_index], dt_raw[layer_idx, seq_index], gate_proj[layer_idx, seq_index], decay_rate[layer_idx], conv_weight[layer_idx], skip_gain[layer_idx], norm_gain[layer_idx])
        previous = lax.map(one_sequence, jnp.arange(SEQS))
        outputs.append(previous)
    return jnp.stack(outputs, axis=0)
```

```python
import functools

import jax
import jax.numpy as jnp
from jax import lax
from jax.experimental import pallas as pl
from jax.experimental.pallas import tpu as pltpu
from jax.sharding import PartitionSpec as P

HEADS = 64
HEAD_DIM = 32
GROUPS = 8
STATE = 64
BLOCK = 128
SEQS = 2
PER_GROUP = HEADS // GROUPS
WIDTH = PER_GROUP * HEAD_DIM
HD = HEADS * HEAD_DIM
UNITS = SEQS * GROUPS
EDGE = 16
TAPS = 4

norm_eps = 1e-05
MESH = pl.DeviceIdType.MESH
HIGHEST = lax.Precision.HIGHEST
STATE_DT = jnp.float32


def silu(v):
    half = 0.5 * v
    return half * jnp.tanh(half) + half


def conv(buf, weight):
    first = EDGE - TAPS + 1
    total = weight[0:1] * buf[first : first + BLOCK]
    for tap in range(1, TAPS):
        total = total + weight[tap : tap + 1] * buf[first + tap : first + tap + BLOCK]
    return silu(total)


def kernel(
    sections,
    ranges,
    x_ref,
    gate_ref,
    bc_ref,
    dt_ref,
    rate_ref,
    w_ref,
    skip_ref,
    gain_ref,
    out_ref,
    weights,
    b_rows,
    c_rows,
    ecum,
    tails,
    cum_cols,
    cum_t,
    dt_t,
    skips,
    cbuf,
    bbuf,
    x_head,
    bc_head,
    prev,
    edge,
    state_in,
    state_out,
    made,
    head_send,
    head_recv,
    prev_send,
    prev_recv,
    edge_send,
    edge_recv,
    state_send,
    state_recv,
):
    f32, bf16 = jnp.float32, jnp.bfloat16
    section = lax.axis_index("pipe")
    mine = lax.axis_index("ctx")
    has_next = section < sections - 1
    has_prev = section > 0
    has_right = mine < ranges - 1
    has_left = mine > 0

    barrier = pltpu.get_barrier_semaphore()
    partners = (
        (has_next, 1, 0),
        (has_next & has_right, 1, 1),
        (has_right, 0, 1),
        (has_prev, -1, 0),
        (has_prev & has_left, -1, -1),
        (has_left, 0, -1),
    )
    count = 0
    for there, down, along in partners:
        count = count + there.astype(jnp.int32)

        @pl.when(there)
        def _(down=down, along=along):
            pl.semaphore_signal(
                barrier,
                inc=1,
                device_id={"pipe": section + down, "ctx": mine + along},
                device_id_type=MESH,
            )

    def head_copy(src, dst, slot):
        return pltpu.make_async_remote_copy(
            src_ref=src.at[0, :, pl.ds(BLOCK - EDGE, EDGE), :],
            dst_ref=dst,
            send_sem=head_send.at[slot],
            recv_sem=head_recv.at[slot],
            device_id={"pipe": section, "ctx": mine + 1},
            device_id_type=MESH,
        )

    def prev_copy(u):
        return pltpu.make_async_remote_copy(
            src_ref=made.at[u],
            dst_ref=prev.at[u],
            send_sem=prev_send.at[u],
            recv_sem=prev_recv.at[u],
            device_id={"pipe": section + 1, "ctx": mine},
            device_id_type=MESH,
        )

    def edge_copy(u):
        return pltpu.make_async_remote_copy(
            src_ref=made.at[u, pl.ds(BLOCK - EDGE, EDGE), :],
            dst_ref=edge.at[u],
            send_sem=edge_send.at[u],
            recv_sem=edge_recv.at[u],
            device_id={"pipe": section + 1, "ctx": mine + 1},
            device_id_type=MESH,
        )

    def state_copy(u):
        return pltpu.make_async_remote_copy(
            src_ref=state_out.at[u],
            dst_ref=state_in.at[u],
            send_sem=state_send.at[u],
            recv_sem=state_recv.at[u],
            device_id={"pipe": section, "ctx": mine + 1},
            device_id_type=MESH,
        )

    pl.semaphore_wait(barrier, count)

    @pl.when(has_right)
    def _():
        head_copy(bc_ref, bc_head, 0).start()
        head_copy(x_ref, x_head, 1).start()

    @pl.when(jnp.logical_not(has_left))
    def _():
        bc_head[...] = jnp.zeros_like(bc_head)
        x_head[...] = jnp.zeros_like(x_head)
        state_in[...] = jnp.zeros_like(state_in)

    @pl.when(jnp.logical_not(has_prev))
    def _():
        prev[...] = jnp.zeros_like(prev)

    @pl.when(jnp.logical_not(has_prev & has_left))
    def _():
        edge[...] = jnp.zeros_like(edge)

    rows = lax.broadcasted_iota(jnp.int32, (BLOCK, BLOCK), 0)
    cols = lax.broadcasted_iota(jnp.int32, (BLOCK, BLOCK), 1)
    lower = rows >= cols
    raw = jnp.concatenate([dt_ref[0, s] for s in range(SEQS)], axis=1)
    steps = jnp.maximum(raw, 0.0) + jnp.log1p(jnp.exp(-jnp.abs(raw)))
    rates = jnp.concatenate([rate_ref[...]] * SEQS, axis=1)
    cum = jnp.dot(
        lower.astype(f32), -steps * rates, precision=HIGHEST, preferred_element_type=f32
    )
    cum_t[...] = cum.T
    dt_t[...] = steps.T
    for u in range(UNITS):
        cum_cols[u] = cum[:, u * PER_GROUP : (u + 1) * PER_GROUP]
    grown = jnp.exp(cum)
    tail = jnp.exp(cum[BLOCK - 1 : BLOCK] - cum) * steps
    both = jnp.concatenate([grown, tail], axis=0)

    sk_rows = lax.broadcasted_iota(jnp.int32, (HEADS, HD), 0)
    sk_cols = lax.broadcasted_iota(jnp.int32, (HEADS, HD), 1)
    skips[...] = jnp.dot(
        jnp.broadcast_to(skip_ref[...], (8, HEADS)),
        (sk_rows == sk_cols // HEAD_DIM).astype(f32),
        precision=HIGHEST,
        preferred_element_type=f32,
    )

    @pl.when(has_left)
    def _():
        head_copy(bc_ref, bc_head, 0).wait_recv()
        head_copy(x_ref, x_head, 1).wait_recv()

    ex_rows = lax.broadcasted_iota(jnp.int32, (BLOCK, WIDTH), 0)
    ex_cols = lax.broadcasted_iota(jnp.int32, (BLOCK, WIDTH), 1)

    def prepare(i, carry):
        s, pair = i // (GROUPS // 2), i % (GROUPS // 2)
        acts = []
        for part in range(2):
            at = pl.multiple_of(part * GROUPS * STATE + pair * 2 * STATE, 2 * STATE)
            bbuf[part, pl.ds(0, EDGE), :] = bc_head[s, :, pl.ds(at, 2 * STATE)].astype(f32)
            bbuf[part, pl.ds(EDGE, BLOCK), :] = bc_ref[0, s, :, pl.ds(at, 2 * STATE)].astype(f32)
            weight = w_ref[0, :, pl.ds(pl.multiple_of(HD + at, 2 * STATE), 2 * STATE)]
            acts.append(conv(bbuf.at[part], weight).astype(bf16))
        b_t = acts[0].astype(f32).T.astype(bf16)
        for half in range(2):
            u = s * GROUPS + pair * 2 + half
            c_u = acts[1][:, half * STATE : (half + 1) * STATE]
            b_u = b_t[half * STATE : (half + 1) * STATE]
            c_rows[u] = c_u
            b_rows[u] = b_u
            scores = jnp.dot(c_u, b_u, preferred_element_type=f32)
            at = pl.multiple_of(u * PER_GROUP, PER_GROUP)
            c_t = cum_t[pl.ds(at, PER_GROUP), :]
            d_t = dt_t[pl.ds(at, PER_GROUP), :]
            c_c = cum_cols[u]
            for h in range(PER_GROUP):
                gap = c_c[:, h : h + 1] - c_t[h : h + 1, :]
                decay = jnp.exp(jnp.where(lower, gap, -1e30))
                weights[u, :, h * BLOCK : (h + 1) * BLOCK] = (
                    scores * decay * d_t[h : h + 1, :]
                ).astype(bf16)
            spread = (ex_rows == u * PER_GROUP + ex_cols // HEAD_DIM).astype(f32)
            wide = jnp.dot(both, spread, precision=HIGHEST, preferred_element_type=f32)
            ecum[u] = wide[:BLOCK]
            tails[u] = wide[BLOCK:]
        return carry

    lax.fori_loop(0, UNITS // 2, prepare, 0)

    lane_head = lax.broadcasted_iota(jnp.int32, (BLOCK, WIDTH), 1) // HEAD_DIM

    def unit(u, carry):
        s, g = u // GROUPS, u % GROUPS
        at = pl.multiple_of(g * WIDTH, WIDTH)
        lanes = pl.ds(at, WIDTH)

        @pl.when(has_prev)
        def _():
            prev_copy(u).wait_recv()

        @pl.when(has_prev & has_left)
        def _():
            edge_copy(u).wait_recv()

        cbuf[pl.ds(0, EDGE), :] = x_head[s, :, lanes].astype(f32) + edge[u].astype(f32)
        cbuf[pl.ds(EDGE, BLOCK), :] = x_ref[0, s, :, lanes].astype(f32) + prev[u].astype(f32)
        xs = conv(cbuf, w_ref[0, :, lanes]).astype(bf16)
        xs32 = xs.astype(f32)
        grow = ecum[u]
        local = jnp.dot(b_rows[u], (xs32 * tails[u]).astype(bf16), preferred_element_type=f32)

        @pl.when(has_left)
        def _():
            state_copy(u).wait_recv()

        incoming = state_in[u].astype(f32)
        state_out[u] = (grow[BLOCK - 1 : BLOCK] * incoming + local).astype(STATE_DT)

        @pl.when(has_right)
        def _():
            state_copy(u).start()

        zero = jnp.zeros_like(xs)
        diagonal = jnp.concatenate(
            [jnp.where(lane_head == h, xs, zero) for h in range(PER_GROUP)], axis=0
        )
        mixed = jnp.dot(weights[u], diagonal, preferred_element_type=f32)
        off = jnp.dot(c_rows[u], incoming.astype(bf16), preferred_element_type=f32)
        mixed = mixed + off * grow + skips[0:1, lanes] * xs32
        gated = mixed * silu(gate_ref[0, s, :, lanes].astype(f32))
        mean = jnp.sum(gated * gated, axis=1, keepdims=True) * (1.0 / WIDTH)
        result = (gated * lax.rsqrt(mean + norm_eps) * gain_ref[0:1, lanes]).astype(bf16)
        made[u] = result

        @pl.when(has_next)
        def _():
            prev_copy(u).start()

        @pl.when(has_next & has_right)
        def _():
            edge_copy(u).start()

        out_ref[0, s, :, lanes] = result
        return carry

    lax.fori_loop(0, UNITS, unit, 0)

    @pl.when(has_right)
    def _():
        head_copy(bc_ref, bc_head, 0).wait_send()
        head_copy(x_ref, x_head, 1).wait_send()

    def drain(u, carry):
        @pl.when(has_right)
        def _():
            state_copy(u).wait_send()

        @pl.when(has_next)
        def _():
            prev_copy(u).wait_send()

        @pl.when(has_next & has_right)
        def _():
            edge_copy(u).wait_send()

        return carry

    lax.fori_loop(0, UNITS, drain, 0)


def solution(mesh):
    sections, ranges = mesh.shape["pipe"], mesh.shape["ctx"]
    f32, bf16 = jnp.float32, jnp.bfloat16
    vmem = pl.BlockSpec(memory_space=pltpu.VMEM)
    dma = pltpu.SemaphoreType.DMA

    def on_device(x, gate, bc, dt, rate, weight, skip, gain):
        return pl.pallas_call(
            functools.partial(kernel, sections, ranges),
            out_shape=jax.ShapeDtypeStruct(x.shape, bf16),
            in_specs=[vmem] * 8,
            out_specs=vmem,
            scratch_shapes=[
                pltpu.VMEM((UNITS, BLOCK, PER_GROUP * BLOCK), bf16),
                pltpu.VMEM((UNITS, STATE, BLOCK), bf16),
                pltpu.VMEM((UNITS, BLOCK, STATE), bf16),
                pltpu.VMEM((UNITS, BLOCK, WIDTH), f32),
                pltpu.VMEM((UNITS, BLOCK, WIDTH), f32),
                pltpu.VMEM((UNITS, BLOCK, PER_GROUP), f32),
                pltpu.VMEM((BLOCK, BLOCK), f32),
                pltpu.VMEM((BLOCK, BLOCK), f32),
                pltpu.VMEM((8, HD), f32),
                pltpu.VMEM((EDGE + BLOCK, WIDTH), f32),
                pltpu.VMEM((2, EDGE + BLOCK, 2 * STATE), f32),
                pltpu.VMEM((SEQS, EDGE, HD), bf16),
                pltpu.VMEM((SEQS, EDGE, 2 * GROUPS * STATE), bf16),
                pltpu.VMEM((UNITS, BLOCK, WIDTH), bf16),
                pltpu.VMEM((UNITS, EDGE, WIDTH), bf16),
                pltpu.VMEM((UNITS, STATE, WIDTH), STATE_DT),
                pltpu.VMEM((UNITS, STATE, WIDTH), STATE_DT),
                pltpu.VMEM((UNITS, BLOCK, WIDTH), bf16),
                dma((2,)),
                dma((2,)),
                dma((UNITS,)),
                dma((UNITS,)),
                dma((UNITS,)),
                dma((UNITS,)),
                dma((UNITS,)),
                dma((UNITS,)),
            ],
            compiler_params=pltpu.CompilerParams(
                collective_id=0, has_side_effects=True, vmem_limit_bytes=48 * 1024 * 1024
            ),
            name="relay",
        )(x, gate, bc, dt, rate, weight, skip, gain)

    rows = P("pipe", None, "ctx", None)
    in_specs = (rows, rows, rows, rows, P("pipe", None), P("pipe", None, None), P("pipe", None), P("pipe", None))
    return jax.shard_map(on_device, mesh=mesh, in_specs=in_specs, out_specs=rows, check_vma=False)
```

```python
import functools

import jax
import jax.numpy as jnp
from jax import lax
from jax.experimental import pallas as pl
from jax.experimental.pallas import tpu as pltpu
from jax.sharding import PartitionSpec as P

HEADS = 64
HEAD_DIM = 32
GROUPS = 8
STATE = 64
BLOCK = 128
SEQS = 2
PER_GROUP = HEADS // GROUPS
WIDTH = PER_GROUP * HEAD_DIM
HD = HEADS * HEAD_DIM
UNITS = SEQS * GROUPS
EDGE = 16
TAPS = 4

norm_eps = 1e-05
MESH = pl.DeviceIdType.MESH
HIGHEST = lax.Precision.HIGHEST
STATE_DT = jnp.bfloat16


def silu(v):
    half = 0.5 * v
    return half * jnp.tanh(half) + half


def conv(buf, weight):
    first = EDGE - TAPS + 1
    total = weight[0:1] * buf[first : first + BLOCK]
    for tap in range(1, TAPS):
        total = total + weight[tap : tap + 1] * buf[first + tap : first + tap + BLOCK]
    return silu(total)


def kernel(
    sections,
    ranges,
    x_hbm,
    gate_hbm,
    bc_hbm,
    dt_ref,
    rate_ref,
    w_ref,
    skip_ref,
    gain_ref,
    out_hbm,
    x_ref,
    gate_ref,
    bc_ref,
    fades,
    weights,
    b_rows,
    c_rows,
    ecum,
    tails,
    cum_cols,
    cum_t,
    dt_t,
    skips,
    cbuf,
    bbuf,
    x_head,
    bc_head,
    prev,
    edge,
    state_in,
    state_out,
    made,
    fetch_sem,
    out_sem,
    head_send,
    head_recv,
    prev_send,
    prev_recv,
    edge_send,
    edge_recv,
    state_send,
    state_recv,
):
    f32, bf16 = jnp.float32, jnp.bfloat16
    section = lax.axis_index("pipe")
    mine = lax.axis_index("ctx")
    has_next = section < sections - 1
    has_prev = section > 0
    has_right = mine < ranges - 1
    has_left = mine > 0

    fetches = [
        pltpu.make_async_copy(src, dst, fetch_sem.at[i])
        for i, (src, dst) in enumerate(((bc_hbm, bc_ref), (x_hbm, x_ref), (gate_hbm, gate_ref)))
    ]
    barrier = pltpu.get_barrier_semaphore()
    partners = (
        (has_next, 1, 0),
        (has_next & has_right, 1, 1),
        (has_right, 0, 1),
        (has_prev, -1, 0),
        (has_prev & has_left, -1, -1),
        (has_left, 0, -1),
    )
    count = 0
    for there, down, along in partners:
        count = count + there.astype(jnp.int32)

        @pl.when(there)
        def _(down=down, along=along):
            pl.semaphore_signal(
                barrier,
                inc=1,
                device_id={"pipe": section + down, "ctx": mine + along},
                device_id_type=MESH,
            )

    def out_copy(u):
        lanes = pl.ds(pl.multiple_of((u % GROUPS) * WIDTH, WIDTH), WIDTH)
        return pltpu.make_async_copy(
            made.at[u], out_hbm.at[0, u // GROUPS, :, lanes], out_sem.at[u]
        )

    def head_copy(src, dst, slot):
        return pltpu.make_async_remote_copy(
            src_ref=src.at[0, :, pl.ds(BLOCK - EDGE, EDGE), :],
            dst_ref=dst,
            send_sem=head_send.at[slot],
            recv_sem=head_recv.at[slot],
            device_id={"pipe": section, "ctx": mine + 1},
            device_id_type=MESH,
        )

    def prev_copy(u):
        return pltpu.make_async_remote_copy(
            src_ref=made.at[u],
            dst_ref=prev.at[u],
            send_sem=prev_send.at[u],
            recv_sem=prev_recv.at[u],
            device_id={"pipe": section + 1, "ctx": mine},
            device_id_type=MESH,
        )

    def edge_copy(u):
        return pltpu.make_async_remote_copy(
            src_ref=made.at[u, pl.ds(BLOCK - EDGE, EDGE), :],
            dst_ref=edge.at[u],
            send_sem=edge_send.at[u],
            recv_sem=edge_recv.at[u],
            device_id={"pipe": section + 1, "ctx": mine + 1},
            device_id_type=MESH,
        )

    def state_copy(u):
        return pltpu.make_async_remote_copy(
            src_ref=state_out.at[u],
            dst_ref=state_in.at[u],
            send_sem=state_send.at[u],
            recv_sem=state_recv.at[u],
            device_id={"pipe": section, "ctx": mine + 1},
            device_id_type=MESH,
        )

    for fetch in fetches:
        fetch.start()

    rows = lax.broadcasted_iota(jnp.int32, (BLOCK, BLOCK), 0)
    cols = lax.broadcasted_iota(jnp.int32, (BLOCK, BLOCK), 1)
    lower = rows >= cols
    raw = jnp.concatenate([dt_ref[0, s] for s in range(SEQS)], axis=0)
    steps = jnp.maximum(raw, 0.0) + jnp.log1p(jnp.exp(-jnp.abs(raw)))
    rates = jnp.concatenate([rate_ref[...]] * SEQS, axis=1)
    rates = jnp.broadcast_to(rates, (BLOCK, SEQS * HEADS)).T
    summed = jnp.dot(
        -steps * rates,
        (rows <= cols).astype(f32),
        precision=HIGHEST,
        preferred_element_type=f32,
    )
    cum_t[...] = summed
    dt_t[...] = steps
    cum = summed.T
    for u in range(UNITS):
        cum_cols[u] = cum[:, u * PER_GROUP : (u + 1) * PER_GROUP]
    grown = jnp.exp(cum)
    tail = jnp.exp(cum[BLOCK - 1 : BLOCK] - cum) * steps.T
    both = jnp.concatenate([grown, tail], axis=0)
    high = both.astype(bf16)
    pair_of = jnp.concatenate([high, (both - high.astype(f32)).astype(bf16)], axis=1)
    ex_rows = lax.broadcasted_iota(jnp.int32, (2 * BLOCK, WIDTH), 0) % BLOCK
    ex_cols = lax.broadcasted_iota(jnp.int32, (2 * BLOCK, WIDTH), 1) // HEAD_DIM

    def fade(u, carry):
        at = pl.multiple_of(u * PER_GROUP, PER_GROUP)
        c_t = cum_t[pl.ds(at, PER_GROUP), :]
        d_t = dt_t[pl.ds(at, PER_GROUP), :]
        c_c = cum_cols[u]
        for h in range(PER_GROUP):
            gap = c_c[:, h : h + 1] - c_t[h : h + 1, :]
            decay = jnp.exp(jnp.where(lower, gap, -1e30))
            fades[u, :, h * BLOCK : (h + 1) * BLOCK] = decay * d_t[h : h + 1, :]
        spread = (ex_rows == u * PER_GROUP + ex_cols).astype(bf16)
        wide = jnp.dot(pair_of, spread, preferred_element_type=f32)
        ecum[u] = wide[:BLOCK]
        tails[u] = wide[BLOCK:]
        return carry

    lax.fori_loop(0, UNITS // 2, fade, 0)

    for fetch in fetches:
        fetch.wait()
    pl.semaphore_wait(barrier, count)

    @pl.when(has_right)
    def _():
        head_copy(bc_ref, bc_head, 0).start()
        head_copy(x_ref, x_head, 1).start()

    @pl.when(jnp.logical_not(has_left))
    def _():
        bc_head[...] = jnp.zeros_like(bc_head)
        x_head[...] = jnp.zeros_like(x_head)
        state_in[...] = jnp.zeros_like(state_in)

    @pl.when(jnp.logical_not(has_prev))
    def _():
        prev[...] = jnp.zeros_like(prev)

    @pl.when(jnp.logical_not(has_prev & has_left))
    def _():
        edge[...] = jnp.zeros_like(edge)

    lax.fori_loop(UNITS // 2, UNITS, fade, 0)

    sk_rows = lax.broadcasted_iota(jnp.int32, (HEADS, HD), 0)
    sk_cols = lax.broadcasted_iota(jnp.int32, (HEADS, HD), 1)
    skips[...] = jnp.dot(
        jnp.broadcast_to(skip_ref[...], (8, HEADS)),
        (sk_rows == sk_cols // HEAD_DIM).astype(f32),
        precision=HIGHEST,
        preferred_element_type=f32,
    )

    @pl.when(has_left)
    def _():
        head_copy(bc_ref, bc_head, 0).wait_recv()
        head_copy(x_ref, x_head, 1).wait_recv()

    def prepare(i, carry):
        s, pair = i // (GROUPS // 2), i % (GROUPS // 2)
        acts = []
        for part in range(2):
            at = pl.multiple_of(part * GROUPS * STATE + pair * 2 * STATE, 2 * STATE)
            bbuf[part, pl.ds(0, EDGE), :] = bc_head[s, :, pl.ds(at, 2 * STATE)].astype(f32)
            bbuf[part, pl.ds(EDGE, BLOCK), :] = bc_ref[0, s, :, pl.ds(at, 2 * STATE)].astype(f32)
            weight = w_ref[0, :, pl.ds(pl.multiple_of(HD + at, 2 * STATE), 2 * STATE)]
            acts.append(conv(bbuf.at[part], weight).astype(bf16))
        b_t = acts[0].astype(f32).T.astype(bf16)
        for half in range(2):
            u = s * GROUPS + pair * 2 + half
            c_u = acts[1][:, half * STATE : (half + 1) * STATE]
            b_u = b_t[half * STATE : (half + 1) * STATE]
            c_rows[u] = c_u
            b_rows[u] = b_u
            scores = jnp.dot(c_u, b_u, preferred_element_type=f32)
            for h in range(PER_GROUP):
                lanes = slice(h * BLOCK, (h + 1) * BLOCK)
                weights[u, :, lanes] = (scores * fades[u, :, lanes]).astype(bf16)
        return carry

    lax.fori_loop(0, UNITS // 2, prepare, 0)

    lane_head = lax.broadcasted_iota(jnp.int32, (BLOCK, WIDTH), 1) // HEAD_DIM

    def unit(u, carry):
        s, g = u // GROUPS, u % GROUPS
        at = pl.multiple_of(g * WIDTH, WIDTH)
        lanes = pl.ds(at, WIDTH)

        @pl.when(has_prev)
        def _():
            prev_copy(u).wait_recv()

        @pl.when(has_prev & has_left)
        def _():
            edge_copy(u).wait_recv()

        cbuf[pl.ds(0, EDGE), :] = x_head[s, :, lanes].astype(f32) + edge[u].astype(f32)
        cbuf[pl.ds(EDGE, BLOCK), :] = x_ref[0, s, :, lanes].astype(f32) + prev[u].astype(f32)
        xs = conv(cbuf, w_ref[0, :, lanes]).astype(bf16)
        xs32 = xs.astype(f32)
        grow = ecum[u]
        local = jnp.dot(b_rows[u], (xs32 * tails[u]).astype(bf16), preferred_element_type=f32)

        @pl.when(has_left)
        def _():
            state_copy(u).wait_recv()

        incoming = state_in[u].astype(f32)
        state_out[u] = (grow[BLOCK - 1 : BLOCK] * incoming + local).astype(STATE_DT)

        @pl.when(has_right)
        def _():
            state_copy(u).start()

        zero = jnp.zeros_like(xs)
        diagonal = jnp.concatenate(
            [jnp.where(lane_head == h, xs, zero) for h in range(PER_GROUP)], axis=0
        )
        mixed = jnp.dot(weights[u], diagonal, preferred_element_type=f32)
        off = jnp.dot(c_rows[u], incoming.astype(bf16), preferred_element_type=f32)
        mixed = mixed + off * grow + skips[0:1, lanes] * xs32
        gated = mixed * silu(gate_ref[0, s, :, lanes].astype(f32))
        mean = jnp.sum(gated * gated, axis=1, keepdims=True) * (1.0 / WIDTH)
        result = (gated * lax.rsqrt(mean + norm_eps) * gain_ref[0:1, lanes]).astype(bf16)
        made[u] = result

        @pl.when(has_next)
        def _():
            prev_copy(u).start()

        @pl.when(has_next & has_right)
        def _():
            edge_copy(u).start()

        out_copy(u).start()
        return carry

    lax.fori_loop(0, UNITS, unit, 0)

    @pl.when(has_right)
    def _():
        head_copy(bc_ref, bc_head, 0).wait_send()
        head_copy(x_ref, x_head, 1).wait_send()

    def drain(u, carry):
        out_copy(u).wait()

        @pl.when(has_right)
        def _():
            state_copy(u).wait_send()

        @pl.when(has_next)
        def _():
            prev_copy(u).wait_send()

        @pl.when(has_next & has_right)
        def _():
            edge_copy(u).wait_send()

        return carry

    lax.fori_loop(0, UNITS, drain, 0)


def solution(mesh):
    sections, ranges = mesh.shape["pipe"], mesh.shape["ctx"]
    f32, bf16 = jnp.float32, jnp.bfloat16
    vmem = pl.BlockSpec(memory_space=pltpu.VMEM)
    hbm = pl.BlockSpec(memory_space=pltpu.HBM)
    dma = pltpu.SemaphoreType.DMA

    def on_device(x, gate, bc, dt, rate, weight, skip, gain):
        return pl.pallas_call(
            functools.partial(kernel, sections, ranges),
            out_shape=jax.ShapeDtypeStruct(x.shape, bf16),
            in_specs=[hbm] * 3 + [vmem] * 5,
            out_specs=hbm,
            scratch_shapes=[
                pltpu.VMEM(x.shape, bf16),
                pltpu.VMEM(gate.shape, bf16),
                pltpu.VMEM(bc.shape, bf16),
                pltpu.VMEM((UNITS, BLOCK, PER_GROUP * BLOCK), f32),
                pltpu.VMEM((UNITS, BLOCK, PER_GROUP * BLOCK), bf16),
                pltpu.VMEM((UNITS, STATE, BLOCK), bf16),
                pltpu.VMEM((UNITS, BLOCK, STATE), bf16),
                pltpu.VMEM((UNITS, BLOCK, WIDTH), f32),
                pltpu.VMEM((UNITS, BLOCK, WIDTH), f32),
                pltpu.VMEM((UNITS, BLOCK, PER_GROUP), f32),
                pltpu.VMEM((BLOCK, BLOCK), f32),
                pltpu.VMEM((BLOCK, BLOCK), f32),
                pltpu.VMEM((8, HD), f32),
                pltpu.VMEM((EDGE + BLOCK, WIDTH), f32),
                pltpu.VMEM((2, EDGE + BLOCK, 2 * STATE), f32),
                pltpu.VMEM((SEQS, EDGE, HD), bf16),
                pltpu.VMEM((SEQS, EDGE, 2 * GROUPS * STATE), bf16),
                pltpu.VMEM((UNITS, BLOCK, WIDTH), bf16),
                pltpu.VMEM((UNITS, EDGE, WIDTH), bf16),
                pltpu.VMEM((UNITS, STATE, WIDTH), STATE_DT),
                pltpu.VMEM((UNITS, STATE, WIDTH), STATE_DT),
                pltpu.VMEM((UNITS, BLOCK, WIDTH), bf16),
                dma((3,)),
                dma((UNITS,)),
                dma((2,)),
                dma((2,)),
                dma((UNITS,)),
                dma((UNITS,)),
                dma((UNITS,)),
                dma((UNITS,)),
                dma((UNITS,)),
                dma((UNITS,)),
            ],
            compiler_params=pltpu.CompilerParams(
                collective_id=0, has_side_effects=True, vmem_limit_bytes=60 * 1024 * 1024
            ),
            name="relay",
        )(x, gate, bc, jnp.swapaxes(dt, 2, 3), rate, weight, skip, gain)

    rows = P("pipe", None, "ctx", None)
    in_specs = (rows, rows, rows, rows, P("pipe", None), P("pipe", None, None), P("pipe", None), P("pipe", None))
    return jax.shard_map(on_device, mesh=mesh, in_specs=in_specs, out_specs=rows, check_vma=False)
```

```python
import functools

import jax
import jax.numpy as jnp
from jax import lax
from jax.experimental import pallas as pl
from jax.experimental.pallas import tpu as pltpu
from jax.sharding import PartitionSpec as P

HEADS = 64
HEAD_DIM = 32
GROUPS = 8
STATE = 64
BLOCK = 128
SEQS = 2
PER_GROUP = HEADS // GROUPS
WIDTH = PER_GROUP * HEAD_DIM
HD = HEADS * HEAD_DIM
UNITS = SEQS * GROUPS
EDGE = 16
KEPT = 4
PAD = 8
TAPS = 4

norm_eps = 1e-05
MESH = pl.DeviceIdType.MESH
HIGHEST = lax.Precision.HIGHEST
STATE_DT = jnp.bfloat16


def silu(v):
    half = 0.5 * v
    return half * jnp.tanh(half) + half


def conv(buf, weight):
    first = PAD - TAPS + 1
    total = weight[0:1] * buf[first : first + BLOCK]
    for tap in range(1, TAPS):
        total = total + weight[tap : tap + 1] * buf[first + tap : first + tap + BLOCK]
    return silu(total)


def kernel(
    sections,
    ranges,
    x_hbm,
    gate_hbm,
    bc_hbm,
    dt_ref,
    rate_ref,
    w_ref,
    skip_ref,
    gain_ref,
    out_ref,
    x_ref,
    gate_ref,
    bc_ref,
    fades,
    weights,
    b_rows,
    c_rows,
    ecum,
    tails,
    cum_cols,
    cum_t,
    dt_t,
    skips,
    cbuf,
    bbuf,
    head_out,
    head_in,
    heads,
    prev,
    edge,
    state_in,
    state_out,
    made,
    fetch_sem,
    head_send,
    head_recv,
    prev_send,
    prev_recv,
    edge_send,
    edge_recv,
    state_send,
    state_recv,
):
    f32, bf16 = jnp.float32, jnp.bfloat16
    section = lax.axis_index("pipe")
    mine = lax.axis_index("ctx")
    has_next = section < sections - 1
    has_prev = section > 0
    has_right = mine < ranges - 1
    has_left = mine > 0

    fetches = [
        pltpu.make_async_copy(src, dst, fetch_sem.at[i])
        for i, (src, dst) in enumerate(((bc_hbm, bc_ref), (x_hbm, x_ref), (gate_hbm, gate_ref)))
    ]
    barrier = pltpu.get_barrier_semaphore()
    partners = (
        (has_next, 1, 0),
        (has_next & has_right, 1, 1),
        (has_right, 0, 1),
        (has_prev, -1, 0),
        (has_prev & has_left, -1, -1),
        (has_left, 0, -1),
    )
    count = 0
    for there, down, along in partners:
        count = count + there.astype(jnp.int32)

        @pl.when(there)
        def _(down=down, along=along):
            pl.semaphore_signal(
                barrier,
                inc=1,
                device_id={"pipe": section + down, "ctx": mine + along},
                device_id_type=MESH,
            )

    def head_copy():
        return pltpu.make_async_remote_copy(
            src_ref=head_out,
            dst_ref=head_in,
            send_sem=head_send,
            recv_sem=head_recv,
            device_id={"pipe": section, "ctx": mine + 1},
            device_id_type=MESH,
        )

    def prev_copy(u):
        return pltpu.make_async_remote_copy(
            src_ref=made.at[u],
            dst_ref=prev.at[u],
            send_sem=prev_send.at[u],
            recv_sem=prev_recv.at[u],
            device_id={"pipe": section + 1, "ctx": mine},
            device_id_type=MESH,
        )

    def edge_copy(u):
        return pltpu.make_async_remote_copy(
            src_ref=made.at[u, pl.ds(BLOCK - EDGE, EDGE), :],
            dst_ref=edge.at[u],
            send_sem=edge_send.at[u],
            recv_sem=edge_recv.at[u],
            device_id={"pipe": section + 1, "ctx": mine + 1},
            device_id_type=MESH,
        )

    def state_copy(u):
        return pltpu.make_async_remote_copy(
            src_ref=state_out.at[u],
            dst_ref=state_in.at[u],
            send_sem=state_send.at[u],
            recv_sem=state_recv.at[u],
            device_id={"pipe": section, "ctx": mine + 1},
            device_id_type=MESH,
        )

    for fetch in fetches:
        fetch.start()

    rows = lax.broadcasted_iota(jnp.int32, (BLOCK, BLOCK), 0)
    cols = lax.broadcasted_iota(jnp.int32, (BLOCK, BLOCK), 1)
    lower = rows >= cols
    raw = jnp.concatenate([dt_ref[0, s] for s in range(SEQS)], axis=0)
    steps = jnp.maximum(raw, 0.0) + jnp.log1p(jnp.exp(-jnp.abs(raw)))
    rates = jnp.concatenate([rate_ref[...]] * SEQS, axis=1)
    rates = jnp.broadcast_to(rates, (BLOCK, SEQS * HEADS)).T
    summed = jnp.dot(
        -steps * rates,
        (rows <= cols).astype(f32),
        precision=HIGHEST,
        preferred_element_type=f32,
    )
    cum_t[...] = summed
    dt_t[...] = steps
    cum = summed.T
    for u in range(UNITS):
        cum_cols[u] = cum[:, u * PER_GROUP : (u + 1) * PER_GROUP]
    grown = jnp.exp(cum)
    tail = jnp.exp(cum[BLOCK - 1 : BLOCK] - cum) * steps.T
    both = jnp.concatenate([grown, tail], axis=0)
    high = both.astype(bf16)
    pair_of = jnp.concatenate([high, (both - high.astype(f32)).astype(bf16)], axis=1)
    ex_rows = lax.broadcasted_iota(jnp.int32, (2 * BLOCK, WIDTH), 0) % BLOCK
    ex_cols = lax.broadcasted_iota(jnp.int32, (2 * BLOCK, WIDTH), 1) // HEAD_DIM

    def fade(u, carry):
        at = pl.multiple_of(u * PER_GROUP, PER_GROUP)
        c_t = cum_t[pl.ds(at, PER_GROUP), :]
        d_t = dt_t[pl.ds(at, PER_GROUP), :]
        c_c = cum_cols[u]
        for h in range(PER_GROUP):
            gap = c_c[:, h : h + 1] - c_t[h : h + 1, :]
            decay = jnp.exp(jnp.where(lower, gap, -1e30))
            fades[u, :, h * BLOCK : (h + 1) * BLOCK] = decay * d_t[h : h + 1, :]
        spread = (ex_rows == u * PER_GROUP + ex_cols).astype(bf16)
        wide = jnp.dot(pair_of, spread, preferred_element_type=f32)
        ecum[u] = wide[:BLOCK]
        tails[u] = wide[BLOCK:]
        return carry

    lax.fori_loop(0, UNITS // 4, fade, 0)

    fetches[0].wait()
    fetches[1].wait()
    for ref, at in ((x_ref, 0), (bc_ref, HD)):
        width = ref.shape[3]
        last = [
            ref[0, s, BLOCK - EDGE :, :].astype(f32)[EDGE - KEPT :] for s in range(SEQS)
        ]
        head_out[:, at : at + width] = jnp.concatenate(last, axis=0).astype(bf16)
    pl.semaphore_wait(barrier, count)

    @pl.when(has_right)
    def _():
        head_copy().start()

    @pl.when(jnp.logical_not(has_left))
    def _():
        head_in[...] = jnp.zeros_like(head_in)
        state_in[...] = jnp.zeros_like(state_in)

    @pl.when(jnp.logical_not(has_prev))
    def _():
        prev[...] = jnp.zeros_like(prev)

    @pl.when(jnp.logical_not(has_prev & has_left))
    def _():
        edge[...] = jnp.zeros_like(edge)

    lax.fori_loop(UNITS // 4, UNITS, fade, 0)

    sk_rows = lax.broadcasted_iota(jnp.int32, (HEADS, HD), 0)
    sk_cols = lax.broadcasted_iota(jnp.int32, (HEADS, HD), 1)
    skips[...] = jnp.dot(
        jnp.broadcast_to(skip_ref[...], (8, HEADS)),
        (sk_rows == sk_cols // HEAD_DIM).astype(f32),
        precision=HIGHEST,
        preferred_element_type=f32,
    )

    @pl.when(has_left)
    def _():
        head_copy().wait_recv()

    arrived = head_in[...].astype(f32)
    for s in range(SEQS):
        heads[s, PAD - KEPT :, :] = arrived[s * KEPT : (s + 1) * KEPT]

    def prepare(i, carry):
        s, pair = i // (GROUPS // 2), i % (GROUPS // 2)
        acts = []
        for part in range(2):
            at = pl.multiple_of(part * GROUPS * STATE + pair * 2 * STATE, 2 * STATE)
            wide = pl.ds(pl.multiple_of(HD + at, 2 * STATE), 2 * STATE)
            bbuf[part, pl.ds(0, PAD), :] = heads[s, :, wide]
            bbuf[part, pl.ds(PAD, BLOCK), :] = bc_ref[0, s, :, pl.ds(at, 2 * STATE)].astype(f32)
            acts.append(conv(bbuf.at[part], w_ref[0, :, wide]).astype(bf16))
        b_t = acts[0].astype(f32).T.astype(bf16)
        for half in range(2):
            u = s * GROUPS + pair * 2 + half
            c_u = acts[1][:, half * STATE : (half + 1) * STATE]
            b_u = b_t[half * STATE : (half + 1) * STATE]
            c_rows[u] = c_u
            b_rows[u] = b_u
            scores = jnp.dot(c_u, b_u, preferred_element_type=f32)
            for h in range(PER_GROUP):
                lanes = slice(h * BLOCK, (h + 1) * BLOCK)
                weights[u, :, lanes] = (scores * fades[u, :, lanes]).astype(bf16)
        return carry

    lax.fori_loop(0, UNITS // 2, prepare, 0)

    fetches[2].wait()
    lane_head = lax.broadcasted_iota(jnp.int32, (BLOCK, WIDTH), 1) // HEAD_DIM

    def unit(u, carry):
        s, g = u // GROUPS, u % GROUPS
        at = pl.multiple_of(g * WIDTH, WIDTH)
        lanes = pl.ds(at, WIDTH)

        @pl.when(has_prev)
        def _():
            prev_copy(u).wait_recv()

        @pl.when(has_prev & has_left)
        def _():
            edge_copy(u).wait_recv()

        cbuf[pl.ds(0, PAD), :] = heads[s, :, lanes] + edge[u].astype(f32)[EDGE - PAD :]
        cbuf[pl.ds(PAD, BLOCK), :] = x_ref[0, s, :, lanes].astype(f32) + prev[u].astype(f32)
        xs = conv(cbuf, w_ref[0, :, lanes]).astype(bf16)
        xs32 = xs.astype(f32)
        grow = ecum[u]
        local = jnp.dot(b_rows[u], (xs32 * tails[u]).astype(bf16), preferred_element_type=f32)

        @pl.when(has_left)
        def _():
            state_copy(u).wait_recv()

        incoming = state_in[u].astype(f32)
        state_out[u] = (grow[BLOCK - 1 : BLOCK] * incoming + local).astype(STATE_DT)

        @pl.when(has_right)
        def _():
            state_copy(u).start()

        zero = jnp.zeros_like(xs)
        diagonal = jnp.concatenate(
            [jnp.where(lane_head == h, xs, zero) for h in range(PER_GROUP)], axis=0
        )
        mixed = jnp.dot(weights[u], diagonal, preferred_element_type=f32)
        off = jnp.dot(c_rows[u], incoming.astype(bf16), preferred_element_type=f32)
        mixed = mixed + off * grow + skips[0:1, lanes] * xs32
        gated = mixed * silu(gate_ref[0, s, :, lanes].astype(f32))
        mean = jnp.sum(gated * gated, axis=1, keepdims=True) * (1.0 / WIDTH)
        result = (gated * lax.rsqrt(mean + norm_eps) * gain_ref[0:1, lanes]).astype(bf16)
        made[u] = result

        @pl.when(has_next)
        def _():
            prev_copy(u).start()

        @pl.when(has_next & has_right)
        def _():
            edge_copy(u).start()

        out_ref[0, s, :, lanes] = result
        return carry

    lax.fori_loop(0, UNITS, unit, 0)

    @pl.when(has_right)
    def _():
        head_copy().wait_send()

    def drain(u, carry):
        @pl.when(has_right)
        def _():
            state_copy(u).wait_send()

        @pl.when(has_next)
        def _():
            prev_copy(u).wait_send()

        @pl.when(has_next & has_right)
        def _():
            edge_copy(u).wait_send()

        return carry

    lax.fori_loop(0, UNITS, drain, 0)


def solution(mesh):
    sections, ranges = mesh.shape["pipe"], mesh.shape["ctx"]
    f32, bf16 = jnp.float32, jnp.bfloat16
    vmem = pl.BlockSpec(memory_space=pltpu.VMEM)
    hbm = pl.BlockSpec(memory_space=pltpu.HBM)
    dma = pltpu.SemaphoreType.DMA
    pin = functools.partial(pltpu.with_memory_space_constraint, memory_space=pltpu.HBM)

    def on_device(x, gate, bc, dt, rate, weight, skip, gain):
        return pl.pallas_call(
            functools.partial(kernel, sections, ranges),
            out_shape=jax.ShapeDtypeStruct(x.shape, bf16),
            in_specs=[hbm] * 3 + [vmem] * 5,
            out_specs=vmem,
            scratch_shapes=[
                pltpu.VMEM(x.shape, bf16),
                pltpu.VMEM(gate.shape, bf16),
                pltpu.VMEM(bc.shape, bf16),
                pltpu.VMEM((UNITS, BLOCK, PER_GROUP * BLOCK), f32),
                pltpu.VMEM((UNITS, BLOCK, PER_GROUP * BLOCK), bf16),
                pltpu.VMEM((UNITS, STATE, BLOCK), bf16),
                pltpu.VMEM((UNITS, BLOCK, STATE), bf16),
                pltpu.VMEM((UNITS, BLOCK, WIDTH), f32),
                pltpu.VMEM((UNITS, BLOCK, WIDTH), f32),
                pltpu.VMEM((UNITS, BLOCK, PER_GROUP), f32),
                pltpu.VMEM((BLOCK, BLOCK), f32),
                pltpu.VMEM((BLOCK, BLOCK), f32),
                pltpu.VMEM((8, HD), f32),
                pltpu.VMEM((PAD + BLOCK, WIDTH), f32),
                pltpu.VMEM((2, PAD + BLOCK, 2 * STATE), f32),
                pltpu.VMEM((SEQS * KEPT, x.shape[3] + bc.shape[3]), bf16),
                pltpu.VMEM((SEQS * KEPT, x.shape[3] + bc.shape[3]), bf16),
                pltpu.VMEM((SEQS, PAD, x.shape[3] + bc.shape[3]), f32),
                pltpu.VMEM((UNITS, BLOCK, WIDTH), bf16),
                pltpu.VMEM((UNITS, EDGE, WIDTH), bf16),
                pltpu.VMEM((UNITS, STATE, WIDTH), STATE_DT),
                pltpu.VMEM((UNITS, STATE, WIDTH), STATE_DT),
                pltpu.VMEM((UNITS, BLOCK, WIDTH), bf16),
                dma((3,)),
                dma(()),
                dma(()),
                dma((UNITS,)),
                dma((UNITS,)),
                dma((UNITS,)),
                dma((UNITS,)),
                dma((UNITS,)),
                dma((UNITS,)),
            ],
            compiler_params=pltpu.CompilerParams(
                collective_id=0, has_side_effects=True, vmem_limit_bytes=48 * 1024 * 1024
            ),
            name="relay",
        )(pin(x), pin(gate), pin(bc), jnp.swapaxes(dt, 2, 3), rate, weight, skip, gain)

    rows = P("pipe", None, "ctx", None)
    in_specs = (rows, rows, rows, rows, P("pipe", None), P("pipe", None, None), P("pipe", None), P("pipe", None))
    return jax.shard_map(on_device, mesh=mesh, in_specs=in_specs, out_specs=rows, check_vma=False)
```

```python
import functools

import jax
import jax.numpy as jnp
from jax import lax
from jax.experimental import pallas as pl
from jax.experimental.pallas import tpu as pltpu
from jax.sharding import PartitionSpec as P

HEADS = 64
HEAD_DIM = 32
GROUPS = 8
STATE = 64
BLOCK = 128
SEQS = 2
PER_GROUP = HEADS // GROUPS
WIDTH = PER_GROUP * HEAD_DIM
HD = HEADS * HEAD_DIM
UNITS = SEQS * GROUPS
EDGE = 16
KEPT = 4
PAD = 8
TAPS = 4

norm_eps = 1e-05
MESH = pl.DeviceIdType.MESH
HIGHEST = lax.Precision.HIGHEST
STATE_DT = jnp.bfloat16


def silu(v):
    half = 0.5 * v
    return half * jnp.tanh(half) + half


def conv(buf, weight):
    first = PAD - TAPS + 1
    total = weight[0:1] * buf[first : first + BLOCK]
    for tap in range(1, TAPS):
        total = total + weight[tap : tap + 1] * buf[first + tap : first + tap + BLOCK]
    return silu(total)


def kernel(
    sections,
    ranges,
    x_hbm,
    gate_hbm,
    bc_hbm,
    dt_hbm,
    rate_hbm,
    w_hbm,
    skip_hbm,
    gain_hbm,
    out_ref,
    dt_ref,
    rate_ref,
    w_ref,
    skip_ref,
    gain_ref,
    x_ref,
    gate_ref,
    bc_ref,
    fades,
    weights,
    b_rows,
    c_rows,
    ecum,
    tails,
    cum_cols,
    cum_t,
    dt_t,
    skips,
    cbuf,
    bbuf,
    head_out,
    head_in,
    heads,
    prev,
    edge,
    state_in,
    state_out,
    made,
    fetch_sem,
    head_send,
    head_recv,
    prev_send,
    prev_recv,
    edge_send,
    edge_recv,
    state_send,
    state_recv,
):
    f32, bf16 = jnp.float32, jnp.bfloat16
    section = lax.axis_index("pipe")
    mine = lax.axis_index("ctx")
    has_next = section < sections - 1
    has_prev = section > 0
    has_right = mine < ranges - 1
    has_left = mine > 0

    fetches = [
        pltpu.make_async_copy(src, dst, fetch_sem.at[i])
        for i, (src, dst) in enumerate(
            (
                (dt_hbm, dt_ref),
                (rate_hbm, rate_ref),
                (bc_hbm, bc_ref),
                (x_hbm, x_ref),
                (w_hbm, w_ref),
                (skip_hbm, skip_ref),
                (gain_hbm, gain_ref),
                (gate_hbm, gate_ref),
            )
        )
    ]
    barrier = pltpu.get_barrier_semaphore()
    partners = (
        (has_next, 1, 0),
        (has_next & has_right, 1, 1),
        (has_right, 0, 1),
        (has_prev, -1, 0),
        (has_prev & has_left, -1, -1),
        (has_left, 0, -1),
    )
    count = 0
    for there, down, along in partners:
        count = count + there.astype(jnp.int32)

        @pl.when(there)
        def _(down=down, along=along):
            pl.semaphore_signal(
                barrier,
                inc=1,
                device_id={"pipe": section + down, "ctx": mine + along},
                device_id_type=MESH,
            )

    def head_copy():
        return pltpu.make_async_remote_copy(
            src_ref=head_out,
            dst_ref=head_in,
            send_sem=head_send,
            recv_sem=head_recv,
            device_id={"pipe": section, "ctx": mine + 1},
            device_id_type=MESH,
        )

    def prev_copy(u):
        return pltpu.make_async_remote_copy(
            src_ref=made.at[u],
            dst_ref=prev.at[u],
            send_sem=prev_send.at[u],
            recv_sem=prev_recv.at[u],
            device_id={"pipe": section + 1, "ctx": mine},
            device_id_type=MESH,
        )

    def edge_copy(u):
        return pltpu.make_async_remote_copy(
            src_ref=made.at[u, pl.ds(BLOCK - EDGE, EDGE), :],
            dst_ref=edge.at[u],
            send_sem=edge_send.at[u],
            recv_sem=edge_recv.at[u],
            device_id={"pipe": section + 1, "ctx": mine + 1},
            device_id_type=MESH,
        )

    def state_copy(u):
        return pltpu.make_async_remote_copy(
            src_ref=state_out.at[u],
            dst_ref=state_in.at[u],
            send_sem=state_send.at[u],
            recv_sem=state_recv.at[u],
            device_id={"pipe": section, "ctx": mine + 1},
            device_id_type=MESH,
        )

    for fetch in fetches:
        fetch.start()

    rows = lax.broadcasted_iota(jnp.int32, (BLOCK, BLOCK), 0)
    cols = lax.broadcasted_iota(jnp.int32, (BLOCK, BLOCK), 1)
    lower = rows >= cols
    fetches[0].wait()
    fetches[1].wait()
    raw = jnp.concatenate([dt_ref[0, s] for s in range(SEQS)], axis=0)
    steps = jnp.maximum(raw, 0.0) + jnp.log1p(jnp.exp(-jnp.abs(raw)))
    rates = jnp.concatenate([rate_ref[...]] * SEQS, axis=1)
    rates = jnp.broadcast_to(rates, (BLOCK, SEQS * HEADS)).T
    summed = jnp.dot(
        -steps * rates,
        (rows <= cols).astype(f32),
        precision=HIGHEST,
        preferred_element_type=f32,
    )
    cum_t[...] = summed
    dt_t[...] = steps
    cum = summed.T
    for u in range(UNITS):
        cum_cols[u] = cum[:, u * PER_GROUP : (u + 1) * PER_GROUP]
    grown = jnp.exp(cum)
    tail = jnp.exp(cum[BLOCK - 1 : BLOCK] - cum) * steps.T
    both = jnp.concatenate([grown, tail], axis=0)
    high = both.astype(bf16)
    pair_of = jnp.concatenate([high, (both - high.astype(f32)).astype(bf16)], axis=1)
    ex_rows = lax.broadcasted_iota(jnp.int32, (2 * BLOCK, WIDTH), 0) % BLOCK
    ex_cols = lax.broadcasted_iota(jnp.int32, (2 * BLOCK, WIDTH), 1) // HEAD_DIM

    def fade(u, carry):
        at = pl.multiple_of(u * PER_GROUP, PER_GROUP)
        c_t = cum_t[pl.ds(at, PER_GROUP), :]
        d_t = dt_t[pl.ds(at, PER_GROUP), :]
        c_c = cum_cols[u]
        for h in range(PER_GROUP):
            gap = c_c[:, h : h + 1] - c_t[h : h + 1, :]
            decay = jnp.exp(jnp.where(lower, gap, -1e30))
            fades[u, :, h * BLOCK : (h + 1) * BLOCK] = decay * d_t[h : h + 1, :]
        spread = (ex_rows == u * PER_GROUP + ex_cols).astype(bf16)
        wide = jnp.dot(pair_of, spread, preferred_element_type=f32)
        ecum[u] = wide[:BLOCK]
        tails[u] = wide[BLOCK:]
        return carry

    lax.fori_loop(0, UNITS // 2, fade, 0)

    fetches[2].wait()
    fetches[3].wait()
    for ref, at in ((x_ref, 0), (bc_ref, HD)):
        width = ref.shape[3]
        last = [
            ref[0, s, BLOCK - EDGE :, :].astype(f32)[EDGE - KEPT :] for s in range(SEQS)
        ]
        head_out[:, at : at + width] = jnp.concatenate(last, axis=0).astype(bf16)
    pl.semaphore_wait(barrier, count)

    @pl.when(has_right)
    def _():
        head_copy().start()

    @pl.when(jnp.logical_not(has_left))
    def _():
        head_in[...] = jnp.zeros_like(head_in)
        state_in[...] = jnp.zeros_like(state_in)

    @pl.when(jnp.logical_not(has_prev))
    def _():
        prev[...] = jnp.zeros_like(prev)

    @pl.when(jnp.logical_not(has_prev & has_left))
    def _():
        edge[...] = jnp.zeros_like(edge)

    lax.fori_loop(UNITS // 2, UNITS, fade, 0)

    for fetch in fetches[4:7]:
        fetch.wait()
    sk_rows = lax.broadcasted_iota(jnp.int32, (HEADS, HD), 0)
    sk_cols = lax.broadcasted_iota(jnp.int32, (HEADS, HD), 1)
    skips[...] = jnp.dot(
        jnp.broadcast_to(skip_ref[...], (8, HEADS)),
        (sk_rows == sk_cols // HEAD_DIM).astype(f32),
        precision=HIGHEST,
        preferred_element_type=f32,
    )

    @pl.when(has_left)
    def _():
        head_copy().wait_recv()

    arrived = head_in[...].astype(f32)
    for s in range(SEQS):
        heads[s, PAD - KEPT :, :] = arrived[s * KEPT : (s + 1) * KEPT]

    def prepare(i, carry):
        s, pair = i // (GROUPS // 2), i % (GROUPS // 2)
        acts = []
        for part in range(2):
            at = pl.multiple_of(part * GROUPS * STATE + pair * 2 * STATE, 2 * STATE)
            wide = pl.ds(pl.multiple_of(HD + at, 2 * STATE), 2 * STATE)
            bbuf[part, pl.ds(0, PAD), :] = heads[s, :, wide]
            bbuf[part, pl.ds(PAD, BLOCK), :] = bc_ref[0, s, :, pl.ds(at, 2 * STATE)].astype(f32)
            acts.append(conv(bbuf.at[part], w_ref[0, :, wide]).astype(bf16))
        b_t = acts[0].astype(f32).T.astype(bf16)
        for half in range(2):
            u = s * GROUPS + pair * 2 + half
            c_u = acts[1][:, half * STATE : (half + 1) * STATE]
            b_u = b_t[half * STATE : (half + 1) * STATE]
            c_rows[u] = c_u
            b_rows[u] = b_u
            scores = jnp.dot(c_u, b_u, preferred_element_type=f32)
            for h in range(PER_GROUP):
                lanes = slice(h * BLOCK, (h + 1) * BLOCK)
                weights[u, :, lanes] = (scores * fades[u, :, lanes]).astype(bf16)
        return carry

    lax.fori_loop(0, UNITS // 2, prepare, 0)

    fetches[7].wait()
    lane_head = lax.broadcasted_iota(jnp.int32, (BLOCK, WIDTH), 1) // HEAD_DIM

    def unit(u, carry):
        s, g = u // GROUPS, u % GROUPS
        at = pl.multiple_of(g * WIDTH, WIDTH)
        lanes = pl.ds(at, WIDTH)

        @pl.when(has_prev)
        def _():
            prev_copy(u).wait_recv()

        @pl.when(has_prev & has_left)
        def _():
            edge_copy(u).wait_recv()

        cbuf[pl.ds(0, PAD), :] = heads[s, :, lanes] + edge[u].astype(f32)[EDGE - PAD :]
        cbuf[pl.ds(PAD, BLOCK), :] = x_ref[0, s, :, lanes].astype(f32) + prev[u].astype(f32)
        xs = conv(cbuf, w_ref[0, :, lanes]).astype(bf16)
        xs32 = xs.astype(f32)
        grow = ecum[u]
        local = jnp.dot(b_rows[u], (xs32 * tails[u]).astype(bf16), preferred_element_type=f32)

        @pl.when(has_left)
        def _():
            state_copy(u).wait_recv()

        incoming = state_in[u].astype(f32)
        state_out[u] = (grow[BLOCK - 1 : BLOCK] * incoming + local).astype(STATE_DT)

        @pl.when(has_right)
        def _():
            state_copy(u).start()

        zero = jnp.zeros_like(xs)
        diagonal = jnp.concatenate(
            [jnp.where(lane_head == h, xs, zero) for h in range(PER_GROUP)], axis=0
        )
        mixed = jnp.dot(weights[u], diagonal, preferred_element_type=f32)
        off = jnp.dot(c_rows[u], incoming.astype(bf16), preferred_element_type=f32)
        mixed = mixed + off * grow + skips[0:1, lanes] * xs32
        gated = mixed * silu(gate_ref[0, s, :, lanes].astype(f32))
        mean = jnp.sum(gated * gated, axis=1, keepdims=True) * (1.0 / WIDTH)
        result = (gated * lax.rsqrt(mean + norm_eps) * gain_ref[0:1, lanes]).astype(bf16)
        made[u] = result

        @pl.when(has_next)
        def _():
            prev_copy(u).start()

        @pl.when(has_next & has_right)
        def _():
            edge_copy(u).start()

        out_ref[0, s, :, lanes] = result
        return carry

    lax.fori_loop(0, UNITS, unit, 0)

    @pl.when(has_right)
    def _():
        head_copy().wait_send()

    def drain(u, carry):
        @pl.when(has_right)
        def _():
            state_copy(u).wait_send()

        @pl.when(has_next)
        def _():
            prev_copy(u).wait_send()

        @pl.when(has_next & has_right)
        def _():
            edge_copy(u).wait_send()

        return carry

    lax.fori_loop(0, UNITS, drain, 0)


def solution(mesh):
    sections, ranges = mesh.shape["pipe"], mesh.shape["ctx"]
    f32, bf16 = jnp.float32, jnp.bfloat16
    vmem = pl.BlockSpec(memory_space=pltpu.VMEM)
    hbm = pl.BlockSpec(memory_space=pltpu.HBM)
    dma = pltpu.SemaphoreType.DMA
    pin = functools.partial(pltpu.with_memory_space_constraint, memory_space=pltpu.HBM)

    def on_device(x, gate, bc, dt, rate, weight, skip, gain):
        return pl.pallas_call(
            functools.partial(kernel, sections, ranges),
            out_shape=jax.ShapeDtypeStruct(x.shape, bf16),
            in_specs=[hbm] * 8,
            out_specs=vmem,
            scratch_shapes=[
                pltpu.VMEM((1, SEQS, HEADS, BLOCK), f32),
                pltpu.VMEM(rate.shape, f32),
                pltpu.VMEM(weight.shape, f32),
                pltpu.VMEM(skip.shape, f32),
                pltpu.VMEM(gain.shape, f32),
                pltpu.VMEM(x.shape, bf16),
                pltpu.VMEM(gate.shape, bf16),
                pltpu.VMEM(bc.shape, bf16),
                pltpu.VMEM((UNITS, BLOCK, PER_GROUP * BLOCK), f32),
                pltpu.VMEM((UNITS, BLOCK, PER_GROUP * BLOCK), bf16),
                pltpu.VMEM((UNITS, STATE, BLOCK), bf16),
                pltpu.VMEM((UNITS, BLOCK, STATE), bf16),
                pltpu.VMEM((UNITS, BLOCK, WIDTH), f32),
                pltpu.VMEM((UNITS, BLOCK, WIDTH), f32),
                pltpu.VMEM((UNITS, BLOCK, PER_GROUP), f32),
                pltpu.VMEM((BLOCK, BLOCK), f32),
                pltpu.VMEM((BLOCK, BLOCK), f32),
                pltpu.VMEM((8, HD), f32),
                pltpu.VMEM((PAD + BLOCK, WIDTH), f32),
                pltpu.VMEM((2, PAD + BLOCK, 2 * STATE), f32),
                pltpu.VMEM((SEQS * KEPT, x.shape[3] + bc.shape[3]), bf16),
                pltpu.VMEM((SEQS * KEPT, x.shape[3] + bc.shape[3]), bf16),
                pltpu.VMEM((SEQS, PAD, x.shape[3] + bc.shape[3]), f32),
                pltpu.VMEM((UNITS, BLOCK, WIDTH), bf16),
                pltpu.VMEM((UNITS, EDGE, WIDTH), bf16),
                pltpu.VMEM((UNITS, STATE, WIDTH), STATE_DT),
                pltpu.VMEM((UNITS, STATE, WIDTH), STATE_DT),
                pltpu.VMEM((UNITS, BLOCK, WIDTH), bf16),
                dma((8,)),
                dma(()),
                dma(()),
                dma((UNITS,)),
                dma((UNITS,)),
                dma((UNITS,)),
                dma((UNITS,)),
                dma((UNITS,)),
                dma((UNITS,)),
            ],
            compiler_params=pltpu.CompilerParams(
                collective_id=0, has_side_effects=True, vmem_limit_bytes=48 * 1024 * 1024
            ),
            name="relay",
        )(*map(pin, (x, gate, bc, jnp.swapaxes(dt, 2, 3), rate, weight, skip, gain)))

    rows = P("pipe", None, "ctx", None)
    in_specs = (rows, rows, rows, rows, P("pipe", None), P("pipe", None, None), P("pipe", None), P("pipe", None))
    return jax.shard_map(on_device, mesh=mesh, in_specs=in_specs, out_specs=rows, check_vma=False)
```
